32 devices in a mesh: groups: 2 (over x), hour: 16 (over z, y, core).
Axes of the slice: x: 2, y: 2, z: 4, core: 2. Of those that a mesh axis runs over, the one named last changes fastest.
Arguments:
- power: float32 [32, 16, 2048], P('groups', 'hour'), parts along dimension 0, may hold values from -3 to 3
- capacity: float32 [4096], P(('groups', 'hour')), parts along dimension 0, may hold values from 0.01 to 20
- flow_dual: float32 [32, 16, 4096], P('groups', 'hour'), parts along dimension 0, may hold values from -3 to 3
- upper_dual: float32 [32, 16, 2048], P('groups', 'hour'), parts along dimension 0, may hold values from 0 to 0.1
- lower_dual: float32 [32, 16, 2048], P('groups', 'hour'), parts along dimension 0, may hold values from 0 to 0.1
- price: float32 [32, 16], P('groups', 'hour'), parts along dimension 0, may hold values from -5 to 5
- load: bfloat16 [32, 16, 512], P('groups', 'hour'), parts along dimension 0, may hold values from -5 to 5
- shift_factors: bfloat16 [4096, 512], replicated, may hold values from -0.25 to 0.25
- line_limit: float32 [4096], replicated, may hold values from 0.5 to 3
- unit_bus: int32 [2048], replicated, may hold values from 0 to 511
- leakage: float32 [2048], replicated, may hold values from 0.015625 to 0.0625
- initial_state: float32 [4096], P('groups'), parts along dimension 0, may hold values from 0 to 10
- power_limit: float32 [2048], replicated, may hold values from 0.5 to 1.5
- capacity_cost: float32 [2048], replicated, may hold values from 0 to 0.1
Outputs:
- new_power: float32 [32, 16, 2048], P('groups', 'hour'), parts along dimension 0
- new_capacity: float32 [4096], P(('groups', 'hour')), parts along dimension 0
- new_flow_dual: float32 [32, 16, 4096], P('groups', 'hour'), parts along dimension 0
- new_upper_dual: float32 [32, 16, 2048], P('groups', 'hour'), parts along dimension 0
- new_lower_dual: float32 [32, 16, 2048], P('groups', 'hour'), parts along dimension 0
The draws below stay inside these ranges and needn't reach their ends.
There are 2 independent parts, one for each index of `groups`. The reference program is written for one: setup_inputs(seed, part) draws one part's arguments, and reference() takes and returns one part's arrays. A program takes and returns all parts, laid end to end along the dimension named above; an argument that names none is the same for every part. Nothing has to cross between parts.
All inputs are finite; a program needn't handle non-finite values.
Results may differ from the reference program's by a relative error of at most 0.00093.
Values sent between devices are 32-bit elements; how exact they have to be, the bound alone decides.
A program may use at most 128 MiB of HBM per device.

```python
import math
import jax
import jax.numpy as jnp
from jax import lax

U = 2048
LINES = 4096
BUSES = 512
SCEN = 16
ITERS = 4
HOURS = 16


def plant(array, own_key, low, largest):
    index_at = [jax.random.randint(jax.random.fold_in(own_key, axis), (), 0, length) for axis, length in enumerate(array.shape)]
    widest = array.shape.index(max(array.shape))
    neighbour = index_at[:widest] + [(index_at[widest] + 1) % array.shape[widest]] + index_at[widest + 1:]
    return array.at[tuple(index_at)].set(low).at[tuple(neighbour)].set(largest)


def steps_of(key, dims, pieces, smallest, largest):
    loudness, own = 1.0, jax.random.fold_in(key, 6)
    for axis_at, blocks in pieces:
        heights = jnp.exp(jax.random.uniform(jax.random.fold_in(own, axis_at), (blocks,), jnp.float32, smallest / len(pieces), largest / len(pieces)))
        loudness = loudness * jnp.repeat(heights, dims[axis_at] // blocks).reshape([-1 if axis == axis_at else 1 for axis in range(len(dims))])
    return loudness


def gaussian(key, shape, width, reach, cuts=(), kind=jnp.bfloat16):
    result = jax.random.normal(key, shape, jnp.float32) * width
    if len(cuts) > 0:
        result = steps_of(key, shape, cuts, -0.22, 0.18) * result
    return jnp.clip(result, min=-reach, max=reach).astype(kind)


def setup_inputs(seed: int = 0, part: int = 0) -> dict:
    arg_keys = jax.random.split(jax.random.key(seed), 15)
    part_splits = jax.random.split(jax.random.fold_in(arg_keys[14], part), 15)
    return {
        "power": gaussian(part_splits[0], (SCEN, HOURS, U), 0.5, 3.0, ((1, 16),), jnp.float32),
        "capacity": jnp.clip(jnp.exp(math.log(20.0) - 7.6009025 * jax.random.uniform(part_splits[1], (U,), jnp.float32) ** steps_of(part_splits[1], (U,), ((0, 16),), -0.2, 0.2)), 0.01, 20.0),
        "flow_dual": gaussian(part_splits[2], (SCEN, HOURS, LINES), 0.5, 3.0, ((1, 16),), jnp.float32),
        "upper_dual": jnp.clip(0.1 * jax.random.uniform(part_splits[3], (SCEN, HOURS, U), jnp.float32) ** steps_of(part_splits[3], (SCEN, HOURS, U), ((1, 16),), -0.2, 0.2), 0.0, 0.1),
        "lower_dual": jnp.clip(0.1 * jax.random.uniform(part_splits[4], (SCEN, HOURS, U), jnp.float32) ** steps_of(part_splits[4], (SCEN, HOURS, U), ((1, 16),), -0.2, 0.2), 0.0, 0.1),
        "price": gaussian(part_splits[5], (SCEN, HOURS), 1.0, 5.0, ((1, 16),), jnp.float32),
        "load": gaussian(part_splits[6], (SCEN, HOURS, BUSES), 1.0, 5.0, ((1, 16),)),
        "shift_factors": gaussian(arg_keys[7], (LINES, BUSES), BUSES ** -0.5, 0.25),
        "line_limit": jnp.clip(jax.random.uniform(arg_keys[8], (LINES,), jnp.float32, 0.5, 3.0), 0.5, 3.0),
        "unit_bus": plant(jax.random.randint(arg_keys[9], (U,), 0, BUSES), jax.random.fold_in(arg_keys[9], 1), 0, BUSES - 1).astype(jnp.int32),
        "leakage": jnp.clip(jnp.exp(jax.random.uniform(arg_keys[10], (U,), jnp.float32, math.log(0.015625), math.log(0.0625))), 0.015625, 0.0625),
        "initial_state": jnp.clip(jax.random.uniform(part_splits[11], (U,), jnp.float32, 0.0, 10.0), 0.0, 10.0),
        "power_limit": jnp.clip(jax.random.uniform(arg_keys[12], (U,), jnp.float32, 0.5, 1.5), 0.5, 1.5),
        "capacity_cost": jnp.clip(jax.random.uniform(arg_keys[13], (U,), jnp.float32, 0.0, 0.1), 0.0, 0.1),
    }


primal_step = 0.05
dual_step = 0.01


def state_forward(field, retain, start):
    def advance(carry, item):
        carry = retain * carry - item
        return carry, carry
    begin = jnp.broadcast_to(start, (field.shape[0], field.shape[2])).astype(jnp.float32)
    final, states = lax.scan(advance, begin, jnp.moveaxis(field, 1, 0))
    return jnp.moveaxis(states, 0, 1)


def state_adjoint(values, retain):
    def advance(carry, item):
        carry = retain * carry + item
        return carry, carry
    begin = jnp.zeros((values.shape[0], values.shape[2]), jnp.float32)
    final, states = lax.scan(advance, begin, jnp.moveaxis(values, 1, 0), reverse=True)
    return jnp.moveaxis(states, 0, 1)


def reference(power, capacity, flow_dual, upper_dual, lower_dual, price, load, shift_factors, line_limit, unit_bus, leakage, initial_state, power_limit, capacity_cost):
    retain = 1.0 - leakage
    incidence = (unit_bus[:, None] == jnp.arange(BUSES, dtype=jnp.int32)[None, :]).astype(jnp.bfloat16)
    for step in range(ITERS):
        bus_dual = jnp.dot(flow_dual.astype(jnp.bfloat16).reshape(-1, LINES), shift_factors, preferred_element_type=jnp.float32).astype(jnp.bfloat16)
        grid_grad = jnp.dot(bus_dual, incidence.T, preferred_element_type=jnp.float32).reshape(SCEN, HOURS, U)
        state_grad = -state_adjoint(upper_dual - lower_dual, retain)
        trial_power = jnp.clip(power - primal_step * (grid_grad + state_grad - price[:, :, None]), -power_limit, power_limit)
        dual_total = jnp.sum(upper_dual, axis=(0, 1))
        trial_capacity = jnp.maximum(capacity - primal_step * (HOURS * capacity_cost - dual_total / SCEN), 0.0)
        power_bar = 2.0 * trial_power - power
        capacity_bar = 2.0 * trial_capacity - capacity
        injection = jnp.dot(power_bar.astype(jnp.bfloat16).reshape(-1, U), incidence, preferred_element_type=jnp.float32)
        injection = (injection - load.astype(jnp.float32).reshape(-1, BUSES)).astype(jnp.bfloat16)
        flows = jnp.dot(injection, shift_factors.T, preferred_element_type=jnp.float32).reshape(SCEN, HOURS, LINES)
        probe = flow_dual + dual_step * flows
        flow_dual = probe - dual_step * jnp.clip(probe / dual_step, -line_limit, line_limit)
        state_bar = state_forward(power_bar, retain, initial_state)
        upper_dual = jnp.maximum(upper_dual + dual_step * (state_bar - capacity_bar), 0.0)
        lower_dual = jnp.maximum(lower_dual - dual_step * state_bar, 0.0)
        power = trial_power
        capacity = trial_capacity
    return power, capacity, flow_dual, upper_dual, lower_dual
```

```python
import functools

import jax
import jax.numpy as jnp
from jax import lax
from jax.experimental import pallas as pl
from jax.experimental.pallas import tpu as pltpu
from jax.sharding import PartitionSpec as P

ITERS = 4

primal_step = 0.05
dual_step = 0.01


def kernel(
    n,
    power_in,
    capacity_in,
    flow_in,
    upper_in,
    lower_in,
    price_in,
    load_in,
    shift_in,
    limit_in,
    bus_in,
    leak_in,
    start_in,
    plimit_in,
    cost_in,
    power_out,
    capacity_out,
    flow_out,
    upper_out,
    lower_out,
    shift,
    inc,
    power,
    grid,
    flow,
    bar16,
    upper,
    lower,
    upper_stage,
    lower_stage,
    adj,
    adj_got,
    bar,
    bar_got,
    send_sems,
    recv_sems,
    shift_sem,
):
    me = lax.axis_index("hour")
    scen, hdev, units = power_in.shape
    lines, buses = shift.shape
    ud = units // n
    hours = hdev * n
    load_shift = pltpu.make_async_copy(shift_in, shift, shift_sem)
    load_shift.start()

    def peer_of(k):
        return lax.rem(me + k, n)

    def from_of(k):
        return lax.rem(me + n - k, n)

    def copy_to(src, dst, channel, peer):
        return pltpu.make_async_remote_copy(
            src_ref=src.at[peer],
            dst_ref=dst.at[me],
            send_sem=send_sems.at[channel, peer],
            recv_sem=recv_sems.at[channel, me],
            device_id={"hour": peer},
            device_id_type=pl.DeviceIdType.MESH,
        )

    def wait_from(dst, channel, source):
        pltpu.make_async_remote_copy(
            src_ref=dst.at[source],
            dst_ref=dst.at[source],
            send_sem=send_sems.at[channel, source],
            recv_sem=recv_sems.at[channel, source],
            device_id={"hour": source},
            device_id_type=pl.DeviceIdType.MESH,
        ).wait_recv()

    def each(count_from, function):
        def step(k, carry):
            function(k)
            return carry

        lax.fori_loop(count_from, n, step, 0)

    def rows_of(ref, lanes):
        return jnp.concatenate([ref[:, j, lanes] for j in range(hdev)], axis=0)

    barrier = pltpu.get_barrier_semaphore()
    each(
        1,
        lambda k: pl.semaphore_signal(
            barrier,
            inc=1,
            device_id={"hour": peer_of(k)},
            device_id_type=pl.DeviceIdType.MESH,
        ),
    )
    for d in range(n):
        lanes = slice(d * ud, (d + 1) * ud)
        upper_stage[d] = rows_of(upper_in, lanes)
        lower_stage[d] = rows_of(lower_in, lanes)
    pl.semaphore_wait(barrier, n - 1)

    def send_first(k):
        copy_to(upper_stage, upper, 0, peer_of(k)).start()
        copy_to(lower_stage, lower, 1, peer_of(k)).start()

    each(1, send_first)
    upper[me] = upper_stage[me]
    lower[me] = lower_stage[me]
    for d in range(n):
        power[d] = rows_of(power_in, slice(d * ud, (d + 1) * ud))
    for j in range(hdev):
        flow[j * scen : (j + 1) * scen, :] = flow_in[:, j, :]
    piece = 128
    names = bus_in[...]
    for b in range(0, buses, piece):
        rows = lax.broadcasted_iota(jnp.int32, (piece, units), 0) + b
        inc[b : b + piece, :] = jnp.where(rows == names, 1.0, 0.0).astype(jnp.bfloat16)
    capacity_out[...] = capacity_in[...]
    retain = 1.0 - leak_in[pl.ds(me, 1), :]
    begin = start_in[pl.ds(me, 1), :]
    cost = cost_in[pl.ds(me, 1), :]
    price = price_in[...]
    load_shift.wait()

    def wait_first(k):
        wait_from(upper, 0, from_of(k))
        wait_from(lower, 1, from_of(k))
        copy_to(upper_stage, upper, 0, peer_of(k)).wait_send()
        copy_to(lower_stage, lower, 1, peer_of(k)).wait_send()

    each(1, wait_first)

    def iteration(step, carry):
        w = jnp.zeros((scen, ud), jnp.float32)
        total = jnp.zeros((scen, ud), jnp.float32)
        for t in reversed(range(hours)):
            d, rows = t // hdev, slice((t % hdev) * scen, (t % hdev + 1) * scen)
            up = upper[d, rows, :]
            w = retain * w + (up - lower[d, rows, :])
            total = total + up
            adj[d, rows, :] = w
        each(1, lambda k: copy_to(adj, adj_got, 2, peer_of(k)).start())
        adj_got[me] = adj[me]
        dual_total = jnp.sum(total, axis=0, keepdims=True)
        capacity = capacity_out[...]
        trial_capacity = jnp.maximum(
            capacity - primal_step * (hours * cost - dual_total / scen), 0.0
        )
        capacity_bar = 2.0 * trial_capacity - capacity
        capacity_out[...] = trial_capacity

        bus_dual = jnp.dot(
            flow[...].astype(jnp.bfloat16), shift[...], preferred_element_type=jnp.float32
        ).astype(jnp.bfloat16)
        grid_grad = jnp.dot(bus_dual, inc[...], preferred_element_type=jnp.float32)
        for d in range(n):
            grid[d] = grid_grad[:, d * ud : (d + 1) * ud]

        def advance(d):
            limit = plimit_in[pl.ds(d, 1), :]
            old = power[d]
            trial = jnp.clip(
                old - primal_step * (grid[d] - adj_got[d] - price), -limit, limit
            )
            bar[d] = 2.0 * trial - old
            power[d] = trial

        advance(me)
        bar_got[me] = bar[me]

        def answer(k):
            source = from_of(k)
            wait_from(adj_got, 2, source)
            advance(source)
            copy_to(bar, bar_got, 3, source).start()

        each(1, answer)
        for d in range(n):
            bar16[:, d * ud : (d + 1) * ud] = bar[d].astype(jnp.bfloat16)
        injection = lax.dot_general(
            bar16[...], inc[...], (((1,), (1,)), ((), ())), preferred_element_type=jnp.float32
        )
        load = jnp.concatenate([load_in[:, j, :] for j in range(hdev)], axis=0)
        injection = (injection - load.astype(jnp.float32)).astype(jnp.bfloat16)
        width = min(1024, lines)
        for c in range(0, lines, width):
            flows = lax.dot_general(
                injection,
                shift[c : c + width, :],
                (((1,), (1,)), ((), ())),
                preferred_element_type=jnp.float32,
            )
            probe = flow[:, c : c + width] + dual_step * flows
            edge = dual_step * limit_in[:, c : c + width]
            flow[:, c : c + width] = probe - jnp.clip(probe, -edge, edge)

        def wait_bar(k):
            wait_from(bar_got, 3, from_of(k))
            copy_to(adj, adj_got, 2, peer_of(k)).wait_send()
            copy_to(bar, bar_got, 3, from_of(k)).wait_send()

        each(1, wait_bar)
        e = jnp.broadcast_to(begin, (scen, ud))
        for t in range(hours):
            d, rows = t // hdev, slice((t % hdev) * scen, (t % hdev + 1) * scen)
            e = retain * e - bar_got[d, rows, :]
            upper[d, rows, :] = jnp.maximum(
                upper[d, rows, :] + dual_step * (e - capacity_bar), 0.0
            )
            lower[d, rows, :] = jnp.maximum(lower[d, rows, :] - dual_step * e, 0.0)
        return carry

    lax.fori_loop(0, ITERS, iteration, 0)

    def send_last(k):
        copy_to(upper, adj_got, 2, peer_of(k)).start()
        copy_to(lower, lower_stage, 0, peer_of(k)).start()

    each(1, send_last)
    adj_got[me] = upper[me]
    lower_stage[me] = lower[me]
    for d in range(n):
        for j in range(hdev):
            power_out[:, j, d * ud : (d + 1) * ud] = power[d, j * scen : (j + 1) * scen, :]
    for j in range(hdev):
        flow_out[:, j, :] = flow[j * scen : (j + 1) * scen, :]

    def wait_last(k):
        wait_from(adj_got, 2, from_of(k))
        wait_from(lower_stage, 0, from_of(k))
        copy_to(upper, adj_got, 2, peer_of(k)).wait_send()
        copy_to(lower, lower_stage, 0, peer_of(k)).wait_send()

    each(1, wait_last)
    for d in range(n):
        for j in range(hdev):
            lanes, rows = slice(d * ud, (d + 1) * ud), slice(j * scen, (j + 1) * scen)
            upper_out[:, j, lanes] = adj_got[d, rows, :]
            lower_out[:, j, lanes] = lower_stage[d, rows, :]


def on_device(
    power,
    capacity,
    flow_dual,
    upper_dual,
    lower_dual,
    price,
    load,
    shift_factors,
    line_limit,
    unit_bus,
    leakage,
    initial_state,
    power_limit,
    capacity_cost,
):
    n = lax.axis_size("hour")
    scen, hdev, units = power.shape
    lines, buses = shift_factors.shape
    ud, rows = units // n, scen * hdev
    block = pltpu.VMEM((n, rows, ud), jnp.float32)
    vmem = pl.BlockSpec(memory_space=pltpu.VMEM)
    anywhere = pl.BlockSpec(memory_space=pl.ANY)
    out = pl.pallas_call(
        functools.partial(kernel, n),
        out_shape=(
            jax.ShapeDtypeStruct(power.shape, jnp.float32),
            jax.ShapeDtypeStruct((1, ud), jnp.float32),
            jax.ShapeDtypeStruct(flow_dual.shape, jnp.float32),
            jax.ShapeDtypeStruct(upper_dual.shape, jnp.float32),
            jax.ShapeDtypeStruct(lower_dual.shape, jnp.float32),
        ),
        in_specs=[vmem] * 7 + [anywhere] + [vmem] * 6,
        out_specs=(vmem,) * 5,
        scratch_shapes=[
            pltpu.VMEM((lines, buses), jnp.bfloat16),
            pltpu.VMEM((buses, units), jnp.bfloat16),
            block,
            block,
            pltpu.VMEM((rows, lines), jnp.float32),
            pltpu.VMEM((rows, units), jnp.bfloat16),
            block,
            block,
            block,
            block,
            block,
            block,
            block,
            block,
            pltpu.SemaphoreType.DMA((4, n)),
            pltpu.SemaphoreType.DMA((4, n)),
            pltpu.SemaphoreType.DMA,
        ],
        compiler_params=pltpu.CompilerParams(
            collective_id=0, has_side_effects=True, vmem_limit_bytes=48 * 1024 * 1024
        ),
    )(
        power,
        capacity.reshape(1, ud),
        flow_dual,
        upper_dual,
        lower_dual,
        price.T.reshape(rows, 1),
        load,
        shift_factors,
        line_limit.reshape(1, lines),
        unit_bus.reshape(1, units),
        leakage.reshape(n, ud),
        initial_state.reshape(n, ud),
        power_limit.reshape(n, ud),
        capacity_cost.reshape(n, ud),
    )
    return (out[0], out[1].reshape(ud), out[2], out[3], out[4])


def solution(mesh):
    return jax.shard_map(
        on_device,
        mesh=mesh,
        in_specs=(
            P("groups", "hour", None),
            P(("groups", "hour")),
            P("groups", "hour", None),
            P("groups", "hour", None),
            P("groups", "hour", None),
            P("groups", "hour"),
            P("groups", "hour", None),
            P(),
            P(),
            P(),
            P(),
            P("groups"),
            P(),
            P(),
        ),
        out_specs=(
            P("groups", "hour", None),
            P(("groups", "hour")),
            P("groups", "hour", None),
            P("groups", "hour", None),
            P("groups", "hour", None),
        ),
        check_vma=False,
    )
```

```python
import functools

import jax
import jax.numpy as jnp
from jax import lax
from jax.experimental import pallas as pl
from jax.experimental.pallas import tpu as pltpu
from jax.sharding import PartitionSpec as P

ITERS = 4

primal_step = 0.05
dual_step = 0.01


def kernel(n, *refs):
    arrived, refs = refs[:14], refs[14:]
    (power_out, capacity_out, flow_out, upper_out, lower_out), refs = refs[:5], refs[5:]
    held, refs = refs[:14], refs[14:]
    (
        power_in,
        capacity_in,
        flow_in,
        upper_in,
        lower_in,
        price_in,
        load_in,
        shift,
        limit_in,
        bus_in,
        leak_in,
        start_in,
        plimit_in,
        cost_in,
    ) = held
    (
        inc,
        power,
        grid,
        flow,
        bar16,
        upper,
        lower,
        upper_stage,
        lower_stage,
        adj,
        adj_got,
        bar,
        bar_got,
        send_sems,
        recv_sems,
        load_sems,
    ) = refs
    me = lax.axis_index("hour")
    scen, hdev, units = power_in.shape
    lines, buses = shift.shape
    ud = units // n
    hours = hdev * n
    loads = [
        pltpu.make_async_copy(src, dst, load_sems.at[i])
        for i, (src, dst) in enumerate(zip(arrived, held))
    ]
    first = (3, 4)
    for i in first:
        loads[i].start()

    def peer_of(k):
        return lax.rem(me + k, n)

    def from_of(k):
        return lax.rem(me + n - k, n)

    def copy_to(src, dst, channel, peer):
        return pltpu.make_async_remote_copy(
            src_ref=src.at[peer],
            dst_ref=dst.at[me],
            send_sem=send_sems.at[channel, peer],
            recv_sem=recv_sems.at[channel, me],
            device_id={"hour": peer},
            device_id_type=pl.DeviceIdType.MESH,
        )

    def wait_from(dst, channel, source):
        pltpu.make_async_remote_copy(
            src_ref=dst.at[source],
            dst_ref=dst.at[source],
            send_sem=send_sems.at[channel, source],
            recv_sem=recv_sems.at[channel, source],
            device_id={"hour": source},
            device_id_type=pl.DeviceIdType.MESH,
        ).wait_recv()

    def each(count_from, function):
        def step(k, carry):
            function(k)
            return carry

        lax.fori_loop(count_from, n, step, 0)

    def rows_of(ref, lanes):
        return jnp.concatenate([ref[:, j, lanes] for j in range(hdev)], axis=0)

    barrier = pltpu.get_barrier_semaphore()
    each(
        1,
        lambda k: pl.semaphore_signal(
            barrier,
            inc=1,
            device_id={"hour": peer_of(k)},
            device_id_type=pl.DeviceIdType.MESH,
        ),
    )
    for i in (9, 0, 2, 7, 1, 5, 6, 8, 10, 11, 12, 13):
        loads[i].start()
    for i in first:
        loads[i].wait()
    for d in range(n):
        lanes = slice(d * ud, (d + 1) * ud)
        upper_stage[d] = rows_of(upper_in, lanes)
        lower_stage[d] = rows_of(lower_in, lanes)
    pl.semaphore_wait(barrier, n - 1)

    def send_first(k):
        copy_to(upper_stage, upper, 0, peer_of(k)).start()
        copy_to(lower_stage, lower, 1, peer_of(k)).start()

    each(1, send_first)
    upper[me] = upper_stage[me]
    lower[me] = lower_stage[me]
    for i in range(14):
        if i not in first and i != 7:
            loads[i].wait()
    for d in range(n):
        power[d] = rows_of(power_in, slice(d * ud, (d + 1) * ud))
    for j in range(hdev):
        flow[j * scen : (j + 1) * scen, :] = flow_in[:, j, :]
    piece = 128
    names = bus_in[...]
    for b in range(0, buses, piece):
        rows = lax.broadcasted_iota(jnp.int32, (piece, units), 0) + b
        inc[b : b + piece, :] = jnp.where(rows == names, 1.0, 0.0).astype(jnp.bfloat16)
    capacity_out[...] = capacity_in[...]
    retain = 1.0 - leak_in[pl.ds(me, 1), :]
    begin = start_in[pl.ds(me, 1), :]
    cost = cost_in[pl.ds(me, 1), :]
    eye = lax.broadcasted_iota(jnp.int32, (scen, scen), 0) == lax.broadcasted_iota(
        jnp.int32, (scen, scen), 1
    )
    price = jnp.concatenate(
        [
            jnp.sum(jnp.where(eye, price_in[j : j + 1, :], 0.0), axis=1, keepdims=True)
            for j in range(hdev)
        ],
        axis=0,
    )
    loads[7].wait()

    def wait_first(k):
        wait_from(upper, 0, from_of(k))
        wait_from(lower, 1, from_of(k))
        copy_to(upper_stage, upper, 0, peer_of(k)).wait_send()
        copy_to(lower_stage, lower, 1, peer_of(k)).wait_send()

    each(1, wait_first)

    def iteration(step, carry):
        w = jnp.zeros((scen, ud), jnp.float32)
        total = jnp.zeros((scen, ud), jnp.float32)
        for t in reversed(range(hours)):
            d, rows = t // hdev, slice((t % hdev) * scen, (t % hdev + 1) * scen)
            up = upper[d, rows, :]
            w = retain * w + (up - lower[d, rows, :])
            total = total + up
            adj[d, rows, :] = w
        each(1, lambda k: copy_to(adj, adj_got, 2, peer_of(k)).start())
        adj_got[me] = adj[me]
        dual_total = jnp.sum(total, axis=0, keepdims=True)
        capacity = capacity_out[...]
        trial_capacity = jnp.maximum(
            capacity - primal_step * (hours * cost - dual_total / scen), 0.0
        )
        capacity_bar = 2.0 * trial_capacity - capacity
        capacity_out[...] = trial_capacity

        bus_dual = jnp.dot(
            flow[...].astype(jnp.bfloat16), shift[...], preferred_element_type=jnp.float32
        ).astype(jnp.bfloat16)
        grid_grad = jnp.dot(bus_dual, inc[...], preferred_element_type=jnp.float32)
        for d in range(n):
            grid[d] = grid_grad[:, d * ud : (d + 1) * ud]

        def advance(d):
            limit = plimit_in[pl.ds(d, 1), :]
            old = power[d]
            trial = jnp.clip(
                old - primal_step * (grid[d] - adj_got[d] - price), -limit, limit
            )
            bar[d] = 2.0 * trial - old
            power[d] = trial

        advance(me)
        bar_got[me] = bar[me]

        def answer(k):
            source = from_of(k)
            wait_from(adj_got, 2, source)
            advance(source)
            copy_to(bar, bar_got, 3, source).start()

        each(1, answer)
        for d in range(n):
            bar16[:, d * ud : (d + 1) * ud] = bar[d].astype(jnp.bfloat16)
        injection = lax.dot_general(
            bar16[...], inc[...], (((1,), (1,)), ((), ())), preferred_element_type=jnp.float32
        )
        load = jnp.concatenate([load_in[j] for j in range(hdev)], axis=0)
        injection = (injection - load.astype(jnp.float32)).astype(jnp.bfloat16)
        width = min(1024, lines)
        for c in range(0, lines, width):
            flows = lax.dot_general(
                injection,
                shift[c : c + width, :],
                (((1,), (1,)), ((), ())),
                preferred_element_type=jnp.float32,
            )
            probe = flow[:, c : c + width] + dual_step * flows
            edge = dual_step * limit_in[:, c : c + width]
            flow[:, c : c + width] = probe - jnp.clip(probe, -edge, edge)

        def wait_bar(k):
            wait_from(bar_got, 3, from_of(k))
            copy_to(adj, adj_got, 2, peer_of(k)).wait_send()
            copy_to(bar, bar_got, 3, from_of(k)).wait_send()

        each(1, wait_bar)
        e = jnp.broadcast_to(begin, (scen, ud))
        for t in range(hours):
            d, rows = t // hdev, slice((t % hdev) * scen, (t % hdev + 1) * scen)
            e = retain * e - bar_got[d, rows, :]
            upper[d, rows, :] = jnp.maximum(
                upper[d, rows, :] + dual_step * (e - capacity_bar), 0.0
            )
            lower[d, rows, :] = jnp.maximum(lower[d, rows, :] - dual_step * e, 0.0)
        return carry

    lax.fori_loop(0, ITERS, iteration, 0)

    def send_last(k):
        copy_to(upper, adj_got, 2, peer_of(k)).start()
        copy_to(lower, lower_stage, 0, peer_of(k)).start()

    each(1, send_last)
    adj_got[me] = upper[me]
    lower_stage[me] = lower[me]
    for d in range(n):
        for j in range(hdev):
            power_out[:, j, d * ud : (d + 1) * ud] = power[d, j * scen : (j + 1) * scen, :]
    for j in range(hdev):
        flow_out[:, j, :] = flow[j * scen : (j + 1) * scen, :]

    def wait_last(k):
        wait_from(adj_got, 2, from_of(k))
        wait_from(lower_stage, 0, from_of(k))
        copy_to(upper, adj_got, 2, peer_of(k)).wait_send()
        copy_to(lower, lower_stage, 0, peer_of(k)).wait_send()

    each(1, wait_last)
    for d in range(n):
        for j in range(hdev):
            lanes, rows = slice(d * ud, (d + 1) * ud), slice(j * scen, (j + 1) * scen)
            upper_out[:, j, lanes] = adj_got[d, rows, :]
            lower_out[:, j, lanes] = lower_stage[d, rows, :]


def store(*refs):
    sems = refs[10]
    copies = [
        pltpu.make_async_copy(refs[i], refs[5 + i], sems.at[i]) for i in (2, 0, 3, 4, 1)
    ]
    for copy in copies:
        copy.start()
    for copy in copies:
        copy.wait()


def on_device(
    power,
    capacity,
    flow_dual,
    upper_dual,
    lower_dual,
    price,
    load,
    shift_factors,
    line_limit,
    unit_bus,
    leakage,
    initial_state,
    power_limit,
    capacity_cost,
):
    n = lax.axis_size("hour")
    scen, hdev, units = power.shape
    lines, buses = shift_factors.shape
    ud, rows = units // n, scen * hdev
    block = pltpu.VMEM((n, rows, ud), jnp.float32)
    vmem = pl.BlockSpec(memory_space=pltpu.VMEM)
    hbm = pl.BlockSpec(memory_space=pltpu.HBM)
    args = (
        power,
        capacity.reshape(1, ud),
        flow_dual,
        upper_dual,
        lower_dual,
        price.T,
        load.transpose(1, 0, 2),
        shift_factors,
        line_limit.reshape(1, lines),
        unit_bus.reshape(1, units),
        leakage.reshape(n, ud),
        initial_state.reshape(n, ud),
        power_limit.reshape(n, ud),
        capacity_cost.reshape(n, ud),
    )
    results = tuple(
        jax.ShapeDtypeStruct(args[i].shape, jnp.float32) for i in range(5)
    )
    out = pl.pallas_call(
        functools.partial(kernel, n),
        out_shape=results,
        in_specs=[hbm] * 14,
        out_specs=(vmem,) * 5,
        scratch_shapes=[pltpu.VMEM(a.shape, a.dtype) for a in args]
        + [
            pltpu.VMEM((buses, units), jnp.bfloat16),
            block,
            block,
            pltpu.VMEM((rows, lines), jnp.float32),
            pltpu.VMEM((rows, units), jnp.bfloat16),
        ]
        + [block] * 8
        + [
            pltpu.SemaphoreType.DMA((4, n)),
            pltpu.SemaphoreType.DMA((4, n)),
            pltpu.SemaphoreType.DMA((14,)),
        ],
        compiler_params=pltpu.CompilerParams(
            collective_id=0, has_side_effects=True, vmem_limit_bytes=48 * 1024 * 1024
        ),
    )(*(pltpu.with_memory_space_constraint(a, pltpu.HBM) for a in args))
    out = pl.pallas_call(
        store,
        out_shape=results,
        in_specs=[vmem] * 5,
        out_specs=(hbm,) * 5,
        scratch_shapes=[pltpu.SemaphoreType.DMA((5,))],
        compiler_params=pltpu.CompilerParams(vmem_limit_bytes=16 * 1024 * 1024),
    )(*out)
    return (out[0], out[1].reshape(ud), out[2], out[3], out[4])


def solution(mesh):
    return jax.shard_map(
        on_device,
        mesh=mesh,
        in_specs=(
            P("groups", "hour", None),
            P(("groups", "hour")),
            P("groups", "hour", None),
            P("groups", "hour", None),
            P("groups", "hour", None),
            P("groups", "hour"),
            P("groups", "hour", None),
            P(),
            P(),
            P(),
            P(),
            P("groups"),
            P(),
            P(),
        ),
        out_specs=(
            P("groups", "hour", None),
            P(("groups", "hour")),
            P("groups", "hour", None),
            P("groups", "hour", None),
            P("groups", "hour", None),
        ),
        check_vma=False,
    )
```

```python
import functools

import jax
import jax.numpy as jnp
from jax import lax
from jax.experimental import pallas as pl
from jax.experimental.pallas import tpu as pltpu
from jax.sharding import PartitionSpec as P

ITERS = 4

primal_step = 0.05
dual_step = 0.01


def kernel(n, *refs):
    arrived, refs = refs[:14], refs[14:]
    (power_out, capacity_out, flow_out, upper_out, lower_out), refs = refs[:5], refs[5:]
    held, refs = refs[:14], refs[14:]
    (
        power_in,
        capacity_in,
        flow_in,
        upper_in,
        lower_in,
        price_in,
        load_in,
        shift,
        limit_in,
        bus_in,
        leak_in,
        start_in,
        plimit_in,
        cost_in,
    ) = held
    (
        inc,
        power,
        grid,
        flow,
        bar16,
        upper,
        lower,
        upper_stage,
        lower_stage,
        adj,
        adj_got,
        bar,
        bar_got,
        send_sems,
        recv_sems,
        load_sems,
    ) = refs
    me = lax.axis_index("hour")
    scen, hdev, units = power_in.shape
    lines, buses = shift.shape
    ud = units // n
    hours = hdev * n
    loads = [
        pltpu.make_async_copy(src, dst, load_sems.at[i])
        for i, (src, dst) in enumerate(zip(arrived, held))
    ]
    first = (3, 4)
    for i in first:
        loads[i].start()

    def peer_of(k):
        return me ^ k

    def copy_to(src, dst, channel, peer):
        return pltpu.make_async_remote_copy(
            src_ref=src.at[peer],
            dst_ref=dst.at[me],
            send_sem=send_sems.at[channel, peer],
            recv_sem=recv_sems.at[channel, me],
            device_id={"hour": peer},
            device_id_type=pl.DeviceIdType.MESH,
        )

    def wait_from(dst, channel, source):
        pltpu.make_async_remote_copy(
            src_ref=dst.at[source],
            dst_ref=dst.at[source],
            send_sem=send_sems.at[channel, source],
            recv_sem=recv_sems.at[channel, source],
            device_id={"hour": source},
            device_id_type=pl.DeviceIdType.MESH,
        ).wait_recv()

    blocks = sorted(range(1, n // 4), key=lambda z: -min(z, n // 4 - z))
    order = [z * 4 + low for low in (2, 3, 0, 1) for z in blocks] + [2, 3, 1]
    assert n % 4 == 0 and n & (n - 1) == 0 and sorted(order) == list(range(1, n))

    def each(order, function):
        for k in order:
            function(k)

    def rows_of(ref, lanes):
        return jnp.concatenate([ref[:, j, lanes] for j in range(hdev)], axis=0)

    barrier = pltpu.get_barrier_semaphore()
    each(
        order,
        lambda k: pl.semaphore_signal(
            barrier,
            inc=1,
            device_id={"hour": peer_of(k)},
            device_id_type=pl.DeviceIdType.MESH,
        ),
    )
    for i in (9, 0, 2, 7, 1, 5, 6, 8, 10, 11, 12, 13):
        loads[i].start()
    for i in first:
        loads[i].wait()
    for d in range(n):
        lanes = slice(d * ud, (d + 1) * ud)
        upper_stage[d] = rows_of(upper_in, lanes)
        lower_stage[d] = upper_stage[d] - rows_of(lower_in, lanes)
    pl.semaphore_wait(barrier, n - 1)

    each(order, lambda k: copy_to(lower_stage, lower, 1, peer_of(k)).start())
    each(order, lambda k: copy_to(upper_stage, upper, 0, peer_of(k)).start())
    upper[me] = upper_stage[me]
    lower[me] = lower_stage[me]
    for i in range(14):
        if i not in first and i != 7:
            loads[i].wait()
    for d in range(n):
        power[d] = rows_of(power_in, slice(d * ud, (d + 1) * ud))
    for j in range(hdev):
        flow[j * scen : (j + 1) * scen, :] = flow_in[:, j, :]
    piece = 128
    names = bus_in[...]
    for b in range(0, buses, piece):
        rows = lax.broadcasted_iota(jnp.int32, (piece, units), 0) + b
        inc[b : b + piece, :] = jnp.where(rows == names, 1.0, 0.0).astype(jnp.bfloat16)
    capacity_out[...] = capacity_in[...]
    retain = 1.0 - leak_in[pl.ds(me, 1), :]
    begin = start_in[pl.ds(me, 1), :]
    cost = cost_in[pl.ds(me, 1), :]
    eye = lax.broadcasted_iota(jnp.int32, (scen, scen), 0) == lax.broadcasted_iota(
        jnp.int32, (scen, scen), 1
    )
    price = jnp.concatenate(
        [
            jnp.sum(jnp.where(eye, price_in[j : j + 1, :], 0.0), axis=1, keepdims=True)
            for j in range(hdev)
        ],
        axis=0,
    )
    loads[7].wait()

    def place(t):
        return t // hdev, slice((t % hdev) * scen, (t % hdev + 1) * scen)

    def adjoint(difference):
        w = jnp.zeros((scen, ud), jnp.float32)
        for t in reversed(range(hours)):
            d, rows = place(t)
            w = retain * w + difference(d, rows)
            adj[d, rows, :] = w
        each(order, lambda k: copy_to(adj, adj_got, 2, peer_of(k)).start())
        adj_got[me] = adj[me]

    def iteration(first):
        bus_dual = jnp.dot(
            flow[...].astype(jnp.bfloat16), shift[...], preferred_element_type=jnp.float32
        ).astype(jnp.bfloat16)
        grid_grad = jnp.dot(bus_dual, inc[...], preferred_element_type=jnp.float32)
        for d in range(n):
            grid[d] = grid_grad[:, d * ud : (d + 1) * ud]

        def advance(d):
            limit = plimit_in[pl.ds(d, 1), :]
            old = power[d]
            trial = jnp.clip(
                old - primal_step * (grid[d] - adj_got[d] - price), -limit, limit
            )
            bar[d] = 2.0 * trial - old
            power[d] = trial

        advance(me)
        bar_got[me] = bar[me]

        def answer(k):
            source = peer_of(k)
            wait_from(adj_got, 2, source)
            advance(source)
            copy_to(bar, bar_got, 3, source).start()

        each(order, answer)
        for d in range(n):
            bar16[:, d * ud : (d + 1) * ud] = bar[d].astype(jnp.bfloat16)
        injection = lax.dot_general(
            bar16[...], inc[...], (((1,), (1,)), ((), ())), preferred_element_type=jnp.float32
        )
        load = jnp.concatenate([load_in[j] for j in range(hdev)], axis=0)
        injection = (injection - load.astype(jnp.float32)).astype(jnp.bfloat16)
        width = min(1024, lines)
        for c in range(0, lines, width):
            flows = lax.dot_general(
                injection,
                shift[c : c + width, :],
                (((1,), (1,)), ((), ())),
                preferred_element_type=jnp.float32,
            )
            probe = flow[:, c : c + width] + dual_step * flows
            edge = dual_step * limit_in[:, c : c + width]
            flow[:, c : c + width] = probe - jnp.clip(probe, -edge, edge)

        if first:

            def wait_upper(k):
                wait_from(upper, 0, peer_of(k))
                copy_to(upper_stage, upper, 0, peer_of(k)).wait_send()
                copy_to(lower_stage, lower, 1, peer_of(k)).wait_send()

            each(order, wait_upper)
            for d in range(n):
                lower[d] = upper[d] - lower[d]
        total = jnp.zeros((scen, ud), jnp.float32)
        for t in range(hours):
            d, rows = place(t)
            total = total + upper[d, rows, :]
        dual_total = jnp.sum(total, axis=0, keepdims=True)
        capacity = capacity_out[...]
        trial_capacity = jnp.maximum(
            capacity - primal_step * (hours * cost - dual_total / scen), 0.0
        )
        capacity_bar = 2.0 * trial_capacity - capacity
        capacity_out[...] = trial_capacity

        def wait_bar(k):
            wait_from(bar_got, 3, peer_of(k))
            copy_to(adj, adj_got, 2, peer_of(k)).wait_send()
            copy_to(bar, bar_got, 3, peer_of(k)).wait_send()

        each(order, wait_bar)
        e = jnp.broadcast_to(begin, (scen, ud))
        for t in range(hours):
            d, rows = place(t)
            e = retain * e - bar_got[d, rows, :]
            upper[d, rows, :] = jnp.maximum(
                upper[d, rows, :] + dual_step * (e - capacity_bar), 0.0
            )
            lower[d, rows, :] = jnp.maximum(lower[d, rows, :] - dual_step * e, 0.0)

    each(order, lambda k: wait_from(lower, 1, peer_of(k)))
    adjoint(lambda d, rows: lower[d, rows, :])
    iteration(True)

    def again(step, carry):
        adjoint(lambda d, rows: upper[d, rows, :] - lower[d, rows, :])
        iteration(False)
        return carry

    lax.fori_loop(1, ITERS, again, 0)

    def send_last(k):
        copy_to(upper, adj_got, 2, peer_of(k)).start()
        copy_to(lower, lower_stage, 0, peer_of(k)).start()

    each(order, send_last)
    adj_got[me] = upper[me]
    lower_stage[me] = lower[me]
    for d in range(n):
        for j in range(hdev):
            power_out[:, j, d * ud : (d + 1) * ud] = power[d, j * scen : (j + 1) * scen, :]
    for j in range(hdev):
        flow_out[:, j, :] = flow[j * scen : (j + 1) * scen, :]

    def wait_last(k):
        wait_from(adj_got, 2, peer_of(k))
        wait_from(lower_stage, 0, peer_of(k))
        copy_to(upper, adj_got, 2, peer_of(k)).wait_send()
        copy_to(lower, lower_stage, 0, peer_of(k)).wait_send()

    each(order, wait_last)
    for d in range(n):
        for j in range(hdev):
            lanes, rows = slice(d * ud, (d + 1) * ud), slice(j * scen, (j + 1) * scen)
            upper_out[:, j, lanes] = adj_got[d, rows, :]
            lower_out[:, j, lanes] = lower_stage[d, rows, :]


def store(*refs):
    sems = refs[10]
    copies = [
        pltpu.make_async_copy(refs[i], refs[5 + i], sems.at[i]) for i in (2, 0, 3, 4, 1)
    ]
    for copy in copies:
        copy.start()
    for copy in copies:
        copy.wait()


def on_device(
    power,
    capacity,
    flow_dual,
    upper_dual,
    lower_dual,
    price,
    load,
    shift_factors,
    line_limit,
    unit_bus,
    leakage,
    initial_state,
    power_limit,
    capacity_cost,
):
    n = lax.axis_size("hour")
    scen, hdev, units = power.shape
    lines, buses = shift_factors.shape
    ud, rows = units // n, scen * hdev
    block = pltpu.VMEM((n, rows, ud), jnp.float32)
    vmem = pl.BlockSpec(memory_space=pltpu.VMEM)
    hbm = pl.BlockSpec(memory_space=pltpu.HBM)
    args = (
        power,
        capacity.reshape(1, ud),
        flow_dual,
        upper_dual,
        lower_dual,
        price.T,
        load.transpose(1, 0, 2),
        shift_factors,
        line_limit.reshape(1, lines),
        unit_bus.reshape(1, units),
        leakage.reshape(n, ud),
        initial_state.reshape(n, ud),
        power_limit.reshape(n, ud),
        capacity_cost.reshape(n, ud),
    )
    results = tuple(
        jax.ShapeDtypeStruct(args[i].shape, jnp.float32) for i in range(5)
    )
    out = pl.pallas_call(
        functools.partial(kernel, n),
        out_shape=results,
        in_specs=[hbm] * 14,
        out_specs=(vmem,) * 5,
        scratch_shapes=[pltpu.VMEM(a.shape, a.dtype) for a in args]
        + [
            pltpu.VMEM((buses, units), jnp.bfloat16),
            block,
            block,
            pltpu.VMEM((rows, lines), jnp.float32),
            pltpu.VMEM((rows, units), jnp.bfloat16),
        ]
        + [block] * 8
        + [
            pltpu.SemaphoreType.DMA((4, n)),
            pltpu.SemaphoreType.DMA((4, n)),
            pltpu.SemaphoreType.DMA((14,)),
        ],
        compiler_params=pltpu.CompilerParams(
            collective_id=0, has_side_effects=True, vmem_limit_bytes=48 * 1024 * 1024
        ),
    )(*(pltpu.with_memory_space_constraint(a, pltpu.HBM) for a in args))
    out = pl.pallas_call(
        store,
        out_shape=results,
        in_specs=[vmem] * 5,
        out_specs=(hbm,) * 5,
        scratch_shapes=[pltpu.SemaphoreType.DMA((5,))],
        compiler_params=pltpu.CompilerParams(vmem_limit_bytes=16 * 1024 * 1024),
    )(*out)
    return (out[0], out[1].reshape(ud), out[2], out[3], out[4])


def solution(mesh):
    return jax.shard_map(
        on_device,
        mesh=mesh,
        in_specs=(
            P("groups", "hour", None),
            P(("groups", "hour")),
            P("groups", "hour", None),
            P("groups", "hour", None),
            P("groups", "hour", None),
            P("groups", "hour"),
            P("groups", "hour", None),
            P(),
            P(),
            P(),
            P(),
            P("groups"),
            P(),
            P(),
        ),
        out_specs=(
            P("groups", "hour", None),
            P(("groups", "hour")),
            P("groups", "hour", None),
            P("groups", "hour", None),
            P("groups", "hour", None),
        ),
        check_vma=False,
    )
```
